32 devices in a mesh: dp: 8 (over y, x, core), seq: 4 (over z).
Axes of the slice: x: 2, y: 2, z: 4, core: 2. Of those that a mesh axis runs over, the one named last changes fastest.
Arguments:
- cond_vec: float32 [8, 3072], P('dp', 'seq'), may hold values from -6 to 6
- mod_weight: bfloat16 [2, 3072, 3072], P(None, 'seq', 'dp'), may hold values from -0.109375 to 0.109375
- text_hidden: bfloat16 [8, 512, 3072], P('dp', 'seq'), may hold values from -121 to 121
- text_grad: bfloat16 [8, 512, 3072], P('dp', 'seq'), may hold values from -14 to 14, as said below
- queries: bfloat16 [8, 2048, 2048], P('dp', 'seq'), may hold values from -4.5 to 4.5
- keys: bfloat16 [8, 2048, 2048], P('dp', 'seq'), may hold values from -4.5 to 4.5
- values: bfloat16 [8, 2048, 2048], P('dp', 'seq'), may hold values from -6 to 6
- out_grad: bfloat16 [8, 2048, 2048], P('dp', 'seq'), may hold values from -6 to 6
Outputs:
- text_hidden_grad: bfloat16 [8, 512, 3072], P('dp', 'seq')
- mod_weight_grad: float32 [2, 3072, 3072], P(None, 'seq', 'dp')
- cond_vec_grad: float32 [8, 3072], P('dp', 'seq')
- query_grad: bfloat16 [8, 2048, 2048], P('dp', 'seq')
- key_grad: bfloat16 [8, 2048, 2048], P('dp', 'seq')
- value_grad: bfloat16 [8, 2048, 2048], P('dp', 'seq')
The draws below stay inside these ranges and needn't reach their ends.
Inputs may be any that keep to these rules, and one draw needn't show every extreme that they name: `text_grad`: incoming gradient.
All inputs are finite; a program needn't handle non-finite values.
Results may differ from the reference program's by a relative error of at most 0.0087.
Values may be sent and summed in bfloat16 or wider, within the bound.
No kernel may reach another device: no remote copies, remote signals or barrier semaphores. Data moves between devices by JAX's collectives and lax.ppermute only.
A program may use at most 128 MiB of HBM per device.

```python
import jax
import jax.numpy as jnp
from jax import lax

D = 3072
HEADS = 16
HEAD_DIM = 128
TXT = 512
JOINT = 2048
BATCH = 8


def drawn_pair(key):
    base = jax.random.fold_in(key, 7)
    first, second = jax.random.split(base, 2)
    width = HEADS * HEAD_DIM
    query = jnp.clip(jax.random.normal(first, (BATCH, JOINT, width), jnp.float32), -4.5, 4.5)
    key_rows = jnp.clip(jax.random.normal(second, (BATCH, JOINT, width), jnp.float32), -4.5, 4.5)
    return (query, key_rows)


def draw_queries(key, part):
    return drawn_pair(key)[0].astype(jnp.bfloat16)


def draw_keys(key, part):
    return drawn_pair(key)[1].astype(jnp.bfloat16)


def draw_text_hidden(key, part):
    first = jax.random.fold_in(jax.random.fold_in(key, 11), 0)
    values_drawn = jnp.clip(jax.random.normal(first, (BATCH, TXT, D), jnp.float32), -6.0, 6.0)
    return values_drawn.astype(jnp.bfloat16)


def draw_text_grad(key, part):
    first = jax.random.fold_in(jax.random.fold_in(key, 13), 0)
    rising = 1.0 + 2.0 * jnp.arange(TXT, dtype=jnp.float32) / (TXT - 1)
    values_drawn = 0.5 * jnp.clip(jax.random.normal(first, (BATCH, TXT, D), jnp.float32), -6.0, 6.0)
    values_drawn = values_drawn * rising[None, :, None]
    return values_drawn.astype(jnp.bfloat16)


def steps_of(rng, shape, pieces, smallest, top_value):
    gain, own = 1.0, jax.random.fold_in(rng, 6)
    for axis_at, shards_of in pieces:
        steps = jnp.exp(jax.random.uniform(jax.random.fold_in(own, axis_at), (shards_of,), jnp.float32, smallest / len(pieces), top_value / len(pieces)))
        gain = gain * jnp.repeat(steps, shape[axis_at] // shards_of).reshape([-1 if axis == axis_at else 1 for axis in range(len(shape))])
    return gain


def normal_values(key, extent, scale, reach, shards=(), kind=jnp.bfloat16):
    level = steps_of(key, extent, shards, -0.22, 0.18) if shards else 1.0
    drawn = jax.random.normal(key, extent, jnp.float32) * scale * level
    return jnp.minimum(jnp.maximum(drawn, -reach), reach).astype(kind)


def setup_inputs(seed: int = 0) -> dict:
    splits = jax.random.split(jax.random.key(seed), 9)
    cond_vec = normal_values(splits[0], (BATCH, D), 1.0, 6.0, ((0, 8), (1, 4)), jnp.float32)
    mod_weight = normal_values(splits[1], (2, D, D), D ** -0.5, 0.109375, ((1, 4), (2, 8)))
    text_hidden = draw_text_hidden(jax.random.fold_in(splits[8], 71), 0)
    text_grad = draw_text_grad(jax.random.fold_in(splits[8], 71), 0)
    queries = draw_queries(jax.random.fold_in(splits[8], 71), 0)
    keys = draw_keys(jax.random.fold_in(splits[8], 71), 0)
    values = normal_values(splits[6], (BATCH, JOINT, HEADS * HEAD_DIM), 1.0, 6.0, ((0, 8), (1, 4)))
    out_grad = normal_values(splits[7], (BATCH, JOINT, HEADS * HEAD_DIM), 1.0, 6.0, ((0, 8), (1, 4)))
    return {"cond_vec": cond_vec, "mod_weight": mod_weight, "text_hidden": text_hidden, "text_grad": text_grad, "queries": queries, "keys": keys, "values": values, "out_grad": out_grad}


norm_eps = 1e-06

def attend_head(arrays):
    query, key_rows, value, grad_out = arrays
    factor = query.shape[-1] ** (-0.5)
    qf = query.astype(jnp.float32)
    kf = key_rows.astype(jnp.float32)
    vf = value.astype(jnp.float32)
    gf = grad_out.astype(jnp.float32)
    scores = jnp.einsum('sd,td->st', qf, kf) * factor
    peak = lax.optimization_barrier(jnp.max(scores, axis=-1, keepdims=True))
    exponent = jnp.exp(scores - peak)
    probability = exponent / lax.optimization_barrier(jnp.sum(exponent, axis=-1, keepdims=True))
    prob_low = lax.optimization_barrier(probability.astype(jnp.bfloat16)).astype(jnp.float32)
    attn_out = jnp.einsum('st,td->sd', prob_low, vf)
    row_delta = lax.optimization_barrier(jnp.sum(gf * attn_out, axis=-1, keepdims=True))
    value_grad = jnp.einsum('st,sd->td', prob_low, gf).astype(jnp.bfloat16)
    prob_grad = jnp.einsum('sd,td->st', gf, vf)
    score_grad = probability * (prob_grad - row_delta) * factor
    score_low = lax.optimization_barrier(score_grad.astype(jnp.bfloat16)).astype(jnp.float32)
    query_grad = jnp.einsum('st,td->sd', score_low, kf).astype(jnp.bfloat16)
    key_grad = jnp.einsum('st,sd->td', score_low, qf).astype(jnp.bfloat16)
    return (query_grad, key_grad, value_grad)

def per_sample(arrays):
    shaped = tuple((a.reshape(JOINT, HEADS, HEAD_DIM).transpose(1, 0, 2) for a in arrays))
    grads = lax.map(attend_head, shaped)
    return tuple((g.transpose(1, 0, 2).reshape(JOINT, HEADS * HEAD_DIM) for g in grads))

def reference(cond_vec, mod_weight, text_hidden, text_grad, queries, keys, values, out_grad):
    act = jax.nn.silu(cond_vec).astype(jnp.bfloat16)
    mod_scale = jnp.dot(act, mod_weight[1], preferred_element_type=jnp.float32)
    hidden = text_hidden.astype(jnp.float32)
    incoming = text_grad.astype(jnp.float32)
    centred = hidden - lax.optimization_barrier(jnp.mean(hidden, axis=-1, keepdims=True))
    inv_std = lax.rsqrt(lax.optimization_barrier(jnp.mean(centred * centred, axis=-1, keepdims=True)) + norm_eps)
    normed = centred * inv_std
    grad_mod = jnp.stack([lax.optimization_barrier(jnp.sum(incoming, axis=1)), lax.optimization_barrier(jnp.sum(incoming * normed, axis=1))], axis=1)
    upstream = incoming * (1.0 + mod_scale[:, None, :])
    text_hidden_grad = inv_std * (upstream - lax.optimization_barrier(jnp.mean(upstream, axis=-1, keepdims=True)) - normed * lax.optimization_barrier(jnp.mean(upstream * normed, axis=-1, keepdims=True)))
    text_hidden_grad = text_hidden_grad.astype(jnp.bfloat16)
    act_wide = act.astype(jnp.float32)
    mod_weight_grad = jnp.einsum('br,bkc->krc', act_wide, grad_mod, precision=lax.Precision.HIGHEST)
    weight_wide = mod_weight.astype(jnp.float32)
    backward = jnp.einsum('bkc,krc->br', grad_mod, weight_wide, precision=lax.Precision.HIGHEST)
    sigma = jax.nn.sigmoid(cond_vec)
    cond_vec_grad = backward * sigma * (1.0 + cond_vec * (1.0 - sigma))
    query_grad, key_grad, value_grad = lax.map(per_sample, (queries, keys, values, out_grad))
    return (text_hidden_grad, mod_weight_grad, cond_vec_grad, query_grad, key_grad, value_grad)
```

```python
import functools
import math

import jax
import jax.numpy as jnp
from jax import lax
from jax.experimental import pallas as pl
from jax.experimental.pallas import tpu as pltpu
from jax.sharding import PartitionSpec as P

HEADS = 16
HEAD_DIM = 128
norm_eps = 1e-06


def fold_rows(array, combine):
    rows, lanes = array.shape
    return combine(array.reshape(rows // 8, 8, lanes), axis=0)


def attend_kernel(parts, rows, width, query_block, key_block, *refs):
    ins, outs = refs[:parts], refs[parts : 2 * parts]
    (q_all, k_all, v_all, g_all, k_flip, q_flip, g_flip, score, prob_grad, key_sum, value_sum,
     query_flip, query_out) = refs[2 * parts :]
    total = parts * rows
    factor = width ** (-0.5)
    scale = factor * math.log2(math.e)
    for part in range(parts):
        here = slice(part * rows, (part + 1) * rows)
        q_all[here, :] = ins[part][0]
        k_all[here, :] = ins[part][1]
        v_all[here, :] = ins[part][2]
        g_all[here, :] = ins[part][3]
        k_flip[:, here] = ins[part][1].T
    key_sum[...] = jnp.zeros_like(key_sum)
    value_sum[...] = jnp.zeros_like(value_sum)

    def one_block(index, _):
        mine = pl.ds(pl.multiple_of(index * query_block, query_block), query_block)
        q_flip[...] = q_all[mine, :].T
        g_flip[...] = g_all[mine, :].T

        def first(step, peak):
            at = pl.ds(pl.multiple_of(step * key_block, key_block), key_block)
            part_score = jnp.dot(k_all[at, :], q_flip[...], preferred_element_type=jnp.float32)
            score[at, :] = part_score
            prob_grad[at, :] = jnp.dot(
                v_all[at, :], g_flip[...], preferred_element_type=jnp.float32
            )
            return jnp.maximum(peak, fold_rows(part_score, jnp.max))

        peak = lax.fori_loop(
            0, total // key_block, first, jnp.full((8, query_block), -jnp.inf, jnp.float32)
        )
        peak = jnp.max(peak, axis=0, keepdims=True)

        def second(step, carry):
            sums, deltas = carry
            at = pl.ds(pl.multiple_of(step * key_block, key_block), key_block)
            exponent = jnp.exp2((score[at, :] - peak) * scale)
            score[at, :] = exponent
            sums = sums + fold_rows(exponent, jnp.sum)
            deltas = deltas + fold_rows(exponent * prob_grad[at, :], jnp.sum)
            return sums, deltas

        empty = jnp.zeros((8, query_block), jnp.float32)
        sums, deltas = lax.fori_loop(0, total // key_block, second, (empty, empty))
        inverse = 1.0 / jnp.sum(sums, axis=0, keepdims=True)
        delta = jnp.sum(deltas, axis=0, keepdims=True) * inverse
        query_flip[...] = jnp.zeros_like(query_flip)

        def third(step, _):
            at = pl.ds(pl.multiple_of(step * key_block, key_block), key_block)
            probability = score[at, :] * inverse
            prob_low = probability.astype(jnp.bfloat16)
            score_low = (probability * (prob_grad[at, :] - delta)).astype(jnp.bfloat16)
            value_sum[at, :] += jnp.dot(
                prob_low, g_all[mine, :], preferred_element_type=jnp.float32
            )
            key_sum[at, :] += jnp.dot(score_low, q_all[mine, :], preferred_element_type=jnp.float32)
            query_flip[...] += jnp.dot(
                k_flip[:, at], score_low, preferred_element_type=jnp.float32
            )
            return 0

        lax.fori_loop(0, total // key_block, third, 0)
        query_out[mine, :] = (query_flip[...] * factor).T.astype(jnp.bfloat16)
        return 0

    lax.fori_loop(0, total // query_block, one_block, 0)
    for part in range(parts):
        here = slice(part * rows, (part + 1) * rows)
        outs[part][0] = query_out[here, :]
        outs[part][1] = (key_sum[here, :] * factor).astype(jnp.bfloat16)
        outs[part][2] = value_sum[here, :].astype(jnp.bfloat16)


def attend(pieces):
    parts = len(pieces)
    _, rows, width = pieces[0].shape
    total = parts * rows
    query_block = math.gcd(total, 512)
    key_block = math.gcd(total, 512)
    low, wide = jnp.bfloat16, jnp.float32
    pairs = total * total
    return pl.pallas_call(
        functools.partial(attend_kernel, parts, rows, width, query_block, key_block),
        out_shape=[jax.ShapeDtypeStruct((3, rows, width), low)] * parts,
        in_specs=[pl.BlockSpec(memory_space=pltpu.VMEM)] * parts,
        out_specs=[pl.BlockSpec(memory_space=pltpu.VMEM)] * parts,
        scratch_shapes=[
            pltpu.VMEM((total, width), low),
            pltpu.VMEM((total, width), low),
            pltpu.VMEM((total, width), low),
            pltpu.VMEM((total, width), low),
            pltpu.VMEM((width, total), low),
            pltpu.VMEM((width, query_block), low),
            pltpu.VMEM((width, query_block), low),
            pltpu.VMEM((total, query_block), wide),
            pltpu.VMEM((total, query_block), wide),
            pltpu.VMEM((total, width), wide),
            pltpu.VMEM((total, width), wide),
            pltpu.VMEM((width, query_block), wide),
            pltpu.VMEM((total, width), low),
        ],
        cost_estimate=pl.CostEstimate(
            flops=10 * pairs * width,
            bytes_accessed=7 * total * width * 2,
            transcendentals=pairs,
        ),
        compiler_params=pltpu.CompilerParams(vmem_limit_bytes=40 * 1024 * 1024),
        name="attend",
    )(*pieces)


def pack_kernel(parts, *refs):
    ins, outs = refs[1 : 1 + 4 * parts], refs[1 + 4 * parts :]
    for part in range(parts):
        for which in range(4):
            outs[part][which] = ins[4 * part + which][...]


def pack(place, arrays, parts, per_device, local):
    rows = arrays[0].shape[0]

    def spec_for(offset):
        return pl.BlockSpec(
            (rows, HEAD_DIM),
            lambda step, at: (0, lax.rem(at[0] + offset, parts) * per_device + local),
        )

    specs = [spec_for(offset) for offset in range(parts) for _ in range(4)]
    shape = (4, rows, HEAD_DIM)
    return pl.pallas_call(
        functools.partial(pack_kernel, parts),
        out_shape=[jax.ShapeDtypeStruct(shape, jnp.bfloat16)] * parts,
        grid_spec=pltpu.PrefetchScalarGridSpec(
            num_scalar_prefetch=1,
            grid=(1,),
            in_specs=specs,
            out_specs=[pl.BlockSpec(shape, lambda step, at: (0, 0, 0))] * parts,
        ),
        cost_estimate=pl.CostEstimate(
            flops=0, bytes_accessed=2 * parts * 4 * rows * HEAD_DIM * 2, transcendentals=0
        ),
        compiler_params=pltpu.CompilerParams(vmem_limit_bytes=24 * 1024 * 1024),
        name="pack",
    )(place, *(list(arrays) * parts))


def unpack_kernel(parts, heads_here, *refs):
    ins, outs = refs[: parts * heads_here], refs[parts * heads_here :]
    for index, piece in enumerate(ins):
        at = slice(index * HEAD_DIM, (index + 1) * HEAD_DIM)
        for which in range(3):
            outs[which][:, at] = piece[which]


def per_device(cond_vec, mod_weight, text_hidden, text_grad, queries, keys, values, out_grad):
    parts = lax.axis_size("seq")
    samples = queries.shape[0]
    heads_here = HEADS // parts
    place = lax.axis_index("seq")
    place_array = jnp.reshape(place, (1,)).astype(jnp.int32)

    def shift(array, offset):
        ring = [(index, (index + offset) % parts) for index in range(parts)]
        return lax.ppermute(array, "seq", ring)

    order = sorted(range(1, parts), key=lambda offset: -min(offset, parts - offset))

    def total_over_seq(array):
        return array + sum(shift(array, offset) for offset in order)

    results = []
    for sample in range(samples):
        arrays = [array[sample] for array in (queries, keys, values, out_grad)]
        arrived = []
        for local in range(heads_here):
            packed = pack(place_array, arrays, parts, heads_here, local)
            pieces = {offset: shift(packed[offset], offset) for offset in order}
            arrived.append([packed[0]] + [pieces[offset] for offset in range(1, parts)])
        back = []
        for local in range(heads_here):
            grads = attend(arrived[local])
            pieces = {offset: shift(grads[offset], parts - offset) for offset in order}
            back.append([grads[0]] + [pieces[offset] for offset in range(1, parts)])
        columns = []
        for offset in range(parts):
            columns.append(jnp.concatenate([back[local][offset] for local in range(heads_here)], axis=2))
        rows, width = queries.shape[1:]
        joined = jnp.zeros((3, rows, width), jnp.bfloat16)
        for offset in range(parts):
            owner = lax.rem(place + offset, parts)
            joined = lax.dynamic_update_slice(
                joined, columns[offset], (0, 0, owner * heads_here * HEAD_DIM)
            )
        results.append(joined)
    query_grad = jnp.stack([joined[0] for joined in results])
    key_grad = jnp.stack([joined[1] for joined in results])
    value_grad = jnp.stack([joined[2] for joined in results])

    hidden = text_hidden.astype(jnp.float32)
    incoming = text_grad.astype(jnp.float32)
    centred = hidden - jnp.mean(hidden, axis=-1, keepdims=True)
    inv_std = lax.rsqrt(jnp.mean(centred * centred, axis=-1, keepdims=True) + norm_eps)
    normed = centred * inv_std
    grad_mod = jnp.stack([jnp.sum(incoming, axis=1), jnp.sum(incoming * normed, axis=1)], axis=1)
    summed_grad = total_over_seq(grad_mod)
    owner_grad = lax.all_to_all(summed_grad, "dp", split_axis=2, concat_axis=0, tiled=True)

    cond_all = lax.all_gather(cond_vec, "dp", axis=0, tiled=True)
    act = jax.nn.silu(cond_all).astype(jnp.bfloat16)
    partial_scale = jnp.dot(act, mod_weight[1], preferred_element_type=jnp.float32)
    own_scale = lax.all_to_all(partial_scale, "dp", split_axis=0, concat_axis=1, tiled=True)
    mod_scale = total_over_seq(own_scale)

    upstream = incoming * (1.0 + mod_scale[:, None, :])
    text_hidden_grad = inv_std * (
        upstream
        - jnp.mean(upstream, axis=-1, keepdims=True)
        - normed * jnp.mean(upstream * normed, axis=-1, keepdims=True)
    )
    text_hidden_grad = text_hidden_grad.astype(jnp.bfloat16)
    mod_weight_grad = jnp.einsum(
        "br,bkc->krc", act.astype(jnp.float32), owner_grad, precision=lax.Precision.HIGHEST
    )
    backward = jnp.einsum(
        "bkc,krc->br", owner_grad, mod_weight.astype(jnp.float32), precision=lax.Precision.HIGHEST
    )
    summed_back = lax.psum_scatter(backward, "dp", scatter_dimension=0, tiled=True)
    sigma = jax.nn.sigmoid(cond_vec)
    cond_vec_grad = summed_back * sigma * (1.0 + cond_vec * (1.0 - sigma))
    return (text_hidden_grad, mod_weight_grad, cond_vec_grad, query_grad, key_grad, value_grad)


def solution(mesh):
    return jax.shard_map(
        per_device,
        mesh=mesh,
        in_specs=(
            P("dp", "seq"),
            P(None, "seq", "dp"),
            P("dp", "seq", None),
            P("dp", "seq", None),
            P("dp", "seq", None),
            P("dp", "seq", None),
            P("dp", "seq", None),
            P("dp", "seq", None),
        ),
        out_specs=(
            P("dp", "seq", None),
            P(None, "seq", "dp"),
            P("dp", "seq"),
            P("dp", "seq", None),
            P("dp", "seq", None),
            P("dp", "seq", None),
        ),
        check_vma=False,
    )
```

```python
import functools
import math

import jax
import jax.numpy as jnp
from jax import lax
from jax.experimental import pallas as pl
from jax.experimental.pallas import tpu as pltpu
from jax.sharding import PartitionSpec as P

HEADS = 16
HEAD_DIM = 128
VMEM_BYTES = 60 * 1024 * 1024
norm_eps = 1e-06


def fold_rows(array, combine):
    rows, lanes = array.shape
    return combine(array.reshape(rows // 8, 8, lanes), axis=0)


def attend_kernel(parts, rows, width, query_block, key_block, *refs):
    ins, outs = refs[:parts], refs[parts : 2 * parts]
    (q_all, k_all, v_all, g_all, k_flip, q_flip, g_flip, score, prob_grad, key_sum, value_sum,
     query_flip, query_out) = refs[2 * parts :]
    total = parts * rows
    factor = width ** (-0.5)
    scale = factor * math.log2(math.e)
    for part in range(parts):
        here = slice(part * rows, (part + 1) * rows)
        q_all[here, :] = ins[part][0]
        k_all[here, :] = ins[part][1]
        v_all[here, :] = ins[part][2]
        g_all[here, :] = ins[part][3]
        k_flip[:, here] = ins[part][1].T
    key_sum[...] = jnp.zeros_like(key_sum)
    value_sum[...] = jnp.zeros_like(value_sum)

    def one_block(index, _):
        mine = pl.ds(pl.multiple_of(index * query_block, query_block), query_block)
        q_flip[...] = q_all[mine, :].T
        g_flip[...] = g_all[mine, :].T

        def first(step, peak):
            at = pl.ds(pl.multiple_of(step * key_block, key_block), key_block)
            part_score = jnp.dot(k_all[at, :], q_flip[...], preferred_element_type=jnp.float32)
            score[at, :] = part_score
            prob_grad[at, :] = jnp.dot(
                v_all[at, :], g_flip[...], preferred_element_type=jnp.float32
            )
            return jnp.maximum(peak, fold_rows(part_score, jnp.max))

        peak = lax.fori_loop(
            0, total // key_block, first, jnp.full((8, query_block), -jnp.inf, jnp.float32)
        )
        peak = jnp.max(peak, axis=0, keepdims=True)

        def second(step, carry):
            sums, deltas = carry
            at = pl.ds(pl.multiple_of(step * key_block, key_block), key_block)
            exponent = jnp.exp2((score[at, :] - peak) * scale)
            score[at, :] = exponent
            sums = sums + fold_rows(exponent, jnp.sum)
            deltas = deltas + fold_rows(exponent * prob_grad[at, :], jnp.sum)
            return sums, deltas

        empty = jnp.zeros((8, query_block), jnp.float32)
        sums, deltas = lax.fori_loop(0, total // key_block, second, (empty, empty))
        inverse = 1.0 / jnp.sum(sums, axis=0, keepdims=True)
        delta = jnp.sum(deltas, axis=0, keepdims=True) * inverse
        query_flip[...] = jnp.zeros_like(query_flip)

        def third(step, _):
            at = pl.ds(pl.multiple_of(step * key_block, key_block), key_block)
            probability = score[at, :] * inverse
            prob_low = probability.astype(jnp.bfloat16)
            score_low = (probability * (prob_grad[at, :] - delta)).astype(jnp.bfloat16)
            value_sum[at, :] += jnp.dot(
                prob_low, g_all[mine, :], preferred_element_type=jnp.float32
            )
            key_sum[at, :] += jnp.dot(score_low, q_all[mine, :], preferred_element_type=jnp.float32)
            query_flip[...] += jnp.dot(
                k_flip[:, at], score_low, preferred_element_type=jnp.float32
            )
            return 0

        lax.fori_loop(0, total // key_block, third, 0)
        query_out[mine, :] = (query_flip[...] * factor).T.astype(jnp.bfloat16)
        return 0

    lax.fori_loop(0, total // query_block, one_block, 0)
    for part in range(parts):
        here = slice(part * rows, (part + 1) * rows)
        outs[part][0] = query_out[here, :]
        outs[part][1] = (key_sum[here, :] * factor).astype(jnp.bfloat16)
        outs[part][2] = value_sum[here, :].astype(jnp.bfloat16)


def attend(pieces):
    parts = len(pieces)
    _, rows, width = pieces[0].shape
    total = parts * rows
    query_block = math.gcd(total, 512)
    key_block = math.gcd(total, 512)
    low, wide = jnp.bfloat16, jnp.float32
    pairs = total * total
    return pl.pallas_call(
        functools.partial(attend_kernel, parts, rows, width, query_block, key_block),
        out_shape=[jax.ShapeDtypeStruct((3, rows, width), low)] * parts,
        in_specs=[pl.BlockSpec(memory_space=pltpu.VMEM)] * parts,
        out_specs=[pl.BlockSpec(memory_space=pltpu.VMEM)] * parts,
        scratch_shapes=[
            pltpu.VMEM((total, width), low),
            pltpu.VMEM((total, width), low),
            pltpu.VMEM((total, width), low),
            pltpu.VMEM((total, width), low),
            pltpu.VMEM((width, total), low),
            pltpu.VMEM((width, query_block), low),
            pltpu.VMEM((width, query_block), low),
            pltpu.VMEM((total, query_block), wide),
            pltpu.VMEM((total, query_block), wide),
            pltpu.VMEM((total, width), wide),
            pltpu.VMEM((total, width), wide),
            pltpu.VMEM((width, query_block), wide),
            pltpu.VMEM((total, width), low),
        ],
        cost_estimate=pl.CostEstimate(
            flops=10 * pairs * width,
            bytes_accessed=7 * total * width * 2,
            transcendentals=pairs,
        ),
        compiler_params=pltpu.CompilerParams(vmem_limit_bytes=VMEM_BYTES),
        name="attend",
    )(*pieces)


def pack_kernel(parts, *refs):
    ins, outs = refs[1 : 1 + 4 * parts], refs[1 + 4 * parts :]
    for part in range(parts):
        for which in range(4):
            outs[part][which] = ins[4 * part + which][...]


def pack(place, arrays, parts, per_device, local):
    rows = arrays[0].shape[0]

    def spec_for(offset):
        return pl.BlockSpec(
            (rows, HEAD_DIM),
            lambda step, at: (0, lax.rem(at[0] + offset, parts) * per_device + local),
        )

    specs = [spec_for(offset) for offset in range(parts) for _ in range(4)]
    shape = (4, rows, HEAD_DIM)
    return pl.pallas_call(
        functools.partial(pack_kernel, parts),
        out_shape=[jax.ShapeDtypeStruct(shape, jnp.bfloat16)] * parts,
        grid_spec=pltpu.PrefetchScalarGridSpec(
            num_scalar_prefetch=1,
            grid=(1,),
            in_specs=specs,
            out_specs=[pl.BlockSpec(shape, lambda step, at: (0, 0, 0))] * parts,
        ),
        cost_estimate=pl.CostEstimate(
            flops=0, bytes_accessed=2 * parts * 4 * rows * HEAD_DIM * 2, transcendentals=0
        ),
        compiler_params=pltpu.CompilerParams(vmem_limit_bytes=VMEM_BYTES),
        name="pack",
    )(place, *(list(arrays) * parts))


def unpack_kernel(parts, *refs):
    ins, outs = refs[1 : 1 + parts], refs[-3:]
    step = pl.program_id(0)
    for part in range(parts):

        @pl.when(step == part)
        def _():
            for which in range(3):
                outs[which][...] = ins[part][which]


def unpack(place, pieces, joined, per_device, local):
    parts = len(pieces)
    _, rows, width = pieces[0].shape
    shape = (3, rows, width)
    out_spec = pl.BlockSpec(
        (rows, width), lambda step, at: (0, lax.rem(at[0] + step, parts) * per_device + local)
    )
    specs = [pl.BlockSpec(shape, lambda step, at: (0, 0, 0))] * parts
    previous = [] if joined is None else list(joined)
    specs += [pl.BlockSpec(memory_space=pl.ANY)] * len(previous)
    return pl.pallas_call(
        functools.partial(unpack_kernel, parts),
        out_shape=[jax.ShapeDtypeStruct((rows, parts * per_device * width), jnp.bfloat16)] * 3,
        grid_spec=pltpu.PrefetchScalarGridSpec(
            num_scalar_prefetch=1, grid=(parts,), in_specs=specs, out_specs=[out_spec] * 3
        ),
        input_output_aliases={1 + parts + which: which for which in range(len(previous))},
        cost_estimate=pl.CostEstimate(
            flops=0, bytes_accessed=2 * parts * 3 * rows * width * 2, transcendentals=0
        ),
        compiler_params=pltpu.CompilerParams(vmem_limit_bytes=VMEM_BYTES),
        name="unpack",
    )(place, *pieces, *previous)


def per_device(cond_vec, mod_weight, text_hidden, text_grad, queries, keys, values, out_grad):
    parts = lax.axis_size("seq")
    samples = queries.shape[0]
    heads_here = HEADS // parts
    place = lax.axis_index("seq")
    place_array = jnp.reshape(place, (1,)).astype(jnp.int32)

    def shift(array, offset):
        ring = [(index, (index + offset) % parts) for index in range(parts)]
        return lax.ppermute(array, "seq", ring)

    order = sorted(range(1, parts), key=lambda offset: -min(offset, parts - offset))

    hidden = text_hidden.astype(jnp.float32)
    incoming = text_grad.astype(jnp.float32)
    centred = hidden - jnp.mean(hidden, axis=-1, keepdims=True)
    inv_std = lax.rsqrt(jnp.mean(centred * centred, axis=-1, keepdims=True) + norm_eps)
    normed = centred * inv_std
    grad_mod = jnp.stack([jnp.sum(incoming, axis=1), jnp.sum(incoming * normed, axis=1)], axis=1)
    grad_parts = [grad_mod] + [shift(grad_mod, offset) for offset in order]

    cond_all = lax.all_gather(cond_vec, "dp", axis=0, tiled=True)
    act = jax.nn.silu(cond_all).astype(jnp.bfloat16)
    partial_scale = jnp.dot(act, mod_weight[1], preferred_element_type=jnp.float32)
    own_scale = lax.all_to_all(partial_scale, "dp", split_axis=0, concat_axis=1, tiled=True)
    scale_parts = [own_scale] + [shift(own_scale, offset) for offset in order]

    work = [(sample, local) for sample in range(samples) for local in range(heads_here)]
    arrived = []
    for sample, local in work:
        arrays = [array[sample] for array in (queries, keys, values, out_grad)]
        packed = pack(place_array, arrays, parts, heads_here, local)
        pieces = {offset: shift(packed[offset], offset) for offset in order}
        arrived.append([packed[0]] + [pieces[offset] for offset in range(1, parts)])
    back = []
    for index in range(len(work)):
        grads = attend(arrived[index])
        pieces = {offset: shift(grads[offset], parts - offset) for offset in order}
        back.append([grads[0]] + [pieces[offset] for offset in range(1, parts)])

    def after(arrays, index):
        if index >= len(back):
            return arrays
        arrays, back[index][0] = lax.optimization_barrier((arrays, back[index][0]))
        return arrays

    grad_parts = after(grad_parts, 0)
    scale_parts = after(scale_parts, 1)
    summed_grad = sum(grad_parts)
    owner_grad = lax.all_to_all(summed_grad, "dp", split_axis=2, concat_axis=0, tiled=True)
    mod_scale = sum(scale_parts)
    text_hidden, text_grad = after((text_hidden, text_grad), 1)
    hidden = text_hidden.astype(jnp.float32)
    incoming = text_grad.astype(jnp.float32)
    centred = hidden - jnp.mean(hidden, axis=-1, keepdims=True)
    inv_std = lax.rsqrt(jnp.mean(centred * centred, axis=-1, keepdims=True) + norm_eps)
    normed = centred * inv_std
    upstream = incoming * (1.0 + mod_scale[:, None, :])
    text_hidden_grad = inv_std * (
        upstream
        - jnp.mean(upstream, axis=-1, keepdims=True)
        - normed * jnp.mean(upstream * normed, axis=-1, keepdims=True)
    )
    text_hidden_grad = text_hidden_grad.astype(jnp.bfloat16)
    mod_weight_grad = jnp.einsum(
        "br,bkc->krc", act.astype(jnp.float32), owner_grad, precision=lax.Precision.HIGHEST
    )
    backward = jnp.einsum(
        "bkc,krc->br", owner_grad, mod_weight.astype(jnp.float32), precision=lax.Precision.HIGHEST
    )
    summed_back = lax.psum_scatter(backward, "dp", scatter_dimension=0, tiled=True)
    sigma = jax.nn.sigmoid(cond_vec)
    cond_vec_grad = summed_back * sigma * (1.0 + cond_vec * (1.0 - sigma))

    joined = [None] * samples
    for index, (sample, local) in enumerate(work):
        joined[sample] = unpack(place_array, back[index], joined[sample], heads_here, local)
    query_grad, key_grad, value_grad = (
        jnp.stack([joined[sample][which] for sample in range(samples)]) for which in range(3)
    )
    return (text_hidden_grad, mod_weight_grad, cond_vec_grad, query_grad, key_grad, value_grad)


def solution(mesh):
    return jax.shard_map(
        per_device,
        mesh=mesh,
        in_specs=(
            P("dp", "seq"),
            P(None, "seq", "dp"),
            P("dp", "seq", None),
            P("dp", "seq", None),
            P("dp", "seq", None),
            P("dp", "seq", None),
            P("dp", "seq", None),
            P("dp", "seq", None),
        ),
        out_specs=(
            P("dp", "seq", None),
            P(None, "seq", "dp"),
            P("dp", "seq"),
            P("dp", "seq", None),
            P("dp", "seq", None),
            P("dp", "seq", None),
        ),
        check_vma=False,
    )
```

```python
import functools
import math

import jax
import jax.numpy as jnp
from jax import lax
from jax.experimental import pallas as pl
from jax.experimental.pallas import tpu as pltpu
from jax.sharding import PartitionSpec as P

HEADS = 16
HEAD_DIM = 128
VMEM_BYTES = 60 * 1024 * 1024
norm_eps = 1e-06


def fold_rows(array, combine):
    rows, lanes = array.shape
    return combine(array.reshape(rows // 8, 8, lanes), axis=0)


def attend_kernel(parts, rows, width, query_block, key_block, *refs):
    ins, outs = refs[:parts], refs[parts : 2 * parts]
    (q_all, k_all, v_all, g_all, k_flip, q_flip, g_flip, score, prob_grad, key_sum, value_sum,
     query_flip, query_out) = refs[2 * parts :]
    total = parts * rows
    factor = width ** (-0.5)
    scale = factor * math.log2(math.e)
    for part in range(parts):
        here = slice(part * rows, (part + 1) * rows)
        q_all[here, :] = ins[part][0]
        k_all[here, :] = ins[part][1]
        v_all[here, :] = ins[part][2]
        g_all[here, :] = ins[part][3]
        k_flip[:, here] = ins[part][1].T
    key_sum[...] = jnp.zeros_like(key_sum)
    value_sum[...] = jnp.zeros_like(value_sum)

    def one_block(index, _):
        mine = pl.ds(pl.multiple_of(index * query_block, query_block), query_block)
        q_flip[...] = q_all[mine, :].T
        g_flip[...] = g_all[mine, :].T

        def first(step, peak):
            at = pl.ds(pl.multiple_of(step * key_block, key_block), key_block)
            part_score = jnp.dot(k_all[at, :], q_flip[...], preferred_element_type=jnp.float32)
            score[at, :] = part_score
            prob_grad[at, :] = jnp.dot(
                v_all[at, :], g_flip[...], preferred_element_type=jnp.float32
            )
            return jnp.maximum(peak, fold_rows(part_score, jnp.max))

        peak = lax.fori_loop(
            0, total // key_block, first, jnp.full((8, query_block), -jnp.inf, jnp.float32)
        )
        peak = jnp.max(peak, axis=0, keepdims=True)

        def second(step, carry):
            sums, deltas = carry
            at = pl.ds(pl.multiple_of(step * key_block, key_block), key_block)
            exponent = jnp.exp2((score[at, :] - peak) * scale)
            score[at, :] = exponent
            sums = sums + fold_rows(exponent, jnp.sum)
            deltas = deltas + fold_rows(exponent * prob_grad[at, :], jnp.sum)
            return sums, deltas

        empty = jnp.zeros((8, query_block), jnp.float32)
        sums, deltas = lax.fori_loop(0, total // key_block, second, (empty, empty))
        inverse = 1.0 / jnp.sum(sums, axis=0, keepdims=True)
        delta = jnp.sum(deltas, axis=0, keepdims=True) * inverse
        query_flip[...] = jnp.zeros_like(query_flip)

        def third(step, _):
            at = pl.ds(pl.multiple_of(step * key_block, key_block), key_block)
            probability = score[at, :] * inverse
            prob_low = probability.astype(jnp.bfloat16)
            score_low = (probability * (prob_grad[at, :] - delta)).astype(jnp.bfloat16)
            value_sum[at, :] += jnp.dot(
                prob_low, g_all[mine, :], preferred_element_type=jnp.float32
            )
            key_sum[at, :] += jnp.dot(score_low, q_all[mine, :], preferred_element_type=jnp.float32)
            query_flip[...] += jnp.dot(
                k_flip[:, at], score_low, preferred_element_type=jnp.float32
            )
            return 0

        lax.fori_loop(0, total // key_block, third, 0)
        query_out[mine, :] = (query_flip[...] * factor).T.astype(jnp.bfloat16)
        return 0

    lax.fori_loop(0, total // query_block, one_block, 0)
    for part in range(parts):
        here = slice(part * rows, (part + 1) * rows)
        outs[part][0] = query_out[here, :]
        outs[part][1] = (key_sum[here, :] * factor).astype(jnp.bfloat16)
        outs[part][2] = value_sum[here, :].astype(jnp.bfloat16)


def attend(pieces):
    parts = len(pieces)
    _, rows, width = pieces[0].shape
    total = parts * rows
    query_block = math.gcd(total, 512)
    key_block = math.gcd(total, 512)
    low, wide = jnp.bfloat16, jnp.float32
    pairs = total * total
    return pl.pallas_call(
        functools.partial(attend_kernel, parts, rows, width, query_block, key_block),
        out_shape=[jax.ShapeDtypeStruct((3, rows, width), low)] * parts,
        in_specs=[pl.BlockSpec(memory_space=pltpu.VMEM)] * parts,
        out_specs=[pl.BlockSpec(memory_space=pltpu.VMEM)] * parts,
        scratch_shapes=[
            pltpu.VMEM((total, width), low),
            pltpu.VMEM((total, width), low),
            pltpu.VMEM((total, width), low),
            pltpu.VMEM((total, width), low),
            pltpu.VMEM((width, total), low),
            pltpu.VMEM((width, query_block), low),
            pltpu.VMEM((width, query_block), low),
            pltpu.VMEM((total, query_block), wide),
            pltpu.VMEM((total, query_block), wide),
            pltpu.VMEM((total, width), wide),
            pltpu.VMEM((total, width), wide),
            pltpu.VMEM((width, query_block), wide),
            pltpu.VMEM((total, width), low),
        ],
        cost_estimate=pl.CostEstimate(
            flops=10 * pairs * width,
            bytes_accessed=7 * total * width * 2,
            transcendentals=pairs,
        ),
        compiler_params=pltpu.CompilerParams(vmem_limit_bytes=VMEM_BYTES),
        name="attend",
    )(*pieces)


def pack_kernel(parts, *refs):
    ins, outs = refs[1 : 1 + 4 * parts], refs[1 + 4 * parts :]
    for part in range(parts):
        for which in range(4):
            outs[part][which] = ins[4 * part + which][...]


def pack(place, arrays, parts, per_device, local):
    rows = arrays[0].shape[0]

    def spec_for(offset):
        return pl.BlockSpec(
            (rows, HEAD_DIM),
            lambda step, at: (0, lax.rem(at[0] + offset, parts) * per_device + local),
        )

    specs = [spec_for(offset) for offset in range(parts) for _ in range(4)]
    shape = (4, rows, HEAD_DIM)
    return pl.pallas_call(
        functools.partial(pack_kernel, parts),
        out_shape=[jax.ShapeDtypeStruct(shape, jnp.bfloat16)] * parts,
        grid_spec=pltpu.PrefetchScalarGridSpec(
            num_scalar_prefetch=1,
            grid=(1,),
            in_specs=specs,
            out_specs=[pl.BlockSpec(shape, lambda step, at: (0, 0, 0))] * parts,
        ),
        cost_estimate=pl.CostEstimate(
            flops=0, bytes_accessed=2 * parts * 4 * rows * HEAD_DIM * 2, transcendentals=0
        ),
        compiler_params=pltpu.CompilerParams(vmem_limit_bytes=VMEM_BYTES),
        name="pack",
    )(place, *(list(arrays) * parts))


def unpack_kernel(parts, *refs):
    ins, outs = refs[1 : 1 + parts], refs[-3:]
    step = pl.program_id(0)
    for part in range(parts):

        @pl.when(step == part)
        def _():
            for which in range(3):
                outs[which][...] = ins[part][which]


def unpack(place, pieces, joined, per_device, local):
    parts = len(pieces)
    _, rows, width = pieces[0].shape
    shape = (3, rows, width)
    out_spec = pl.BlockSpec(
        (rows, width), lambda step, at: (0, lax.rem(at[0] + step, parts) * per_device + local)
    )
    specs = [pl.BlockSpec(shape, lambda step, at: (0, 0, 0))] * parts
    previous = [] if joined is None else list(joined)
    specs += [pl.BlockSpec(memory_space=pl.ANY)] * len(previous)
    return pl.pallas_call(
        functools.partial(unpack_kernel, parts),
        out_shape=[jax.ShapeDtypeStruct((rows, parts * per_device * width), jnp.bfloat16)] * 3,
        grid_spec=pltpu.PrefetchScalarGridSpec(
            num_scalar_prefetch=1, grid=(parts,), in_specs=specs, out_specs=[out_spec] * 3
        ),
        input_output_aliases={1 + parts + which: which for which in range(len(previous))},
        cost_estimate=pl.CostEstimate(
            flops=0, bytes_accessed=2 * parts * 3 * rows * width * 2, transcendentals=0
        ),
        compiler_params=pltpu.CompilerParams(vmem_limit_bytes=VMEM_BYTES),
        name="unpack",
    )(place, *pieces, *previous)


def per_device(cond_vec, mod_weight, text_hidden, text_grad, queries, keys, values, out_grad):
    parts = lax.axis_size("seq")
    samples = queries.shape[0]
    heads_here = HEADS // parts
    place = lax.axis_index("seq")
    place_array = jnp.reshape(place, (1,)).astype(jnp.int32)

    def shift(array, offset):
        ring = [(index, (index + offset) % parts) for index in range(parts)]
        return lax.ppermute(array, "seq", ring)

    order = sorted(range(1, parts), key=lambda offset: -min(offset, parts - offset))

    hidden = text_hidden.astype(jnp.float32)
    incoming = text_grad.astype(jnp.float32)
    centred = hidden - jnp.mean(hidden, axis=-1, keepdims=True)
    inv_std = lax.rsqrt(jnp.mean(centred * centred, axis=-1, keepdims=True) + norm_eps)
    normed = centred * inv_std
    grad_mod = jnp.stack([jnp.sum(incoming, axis=1), jnp.sum(incoming * normed, axis=1)], axis=1)
    grad_parts = [grad_mod] + [shift(grad_mod, offset) for offset in order]

    cond_all = lax.all_gather(cond_vec, "dp", axis=0, tiled=True)
    act = jax.nn.silu(cond_all).astype(jnp.bfloat16)
    partial_scale = jnp.dot(act, mod_weight[1], preferred_element_type=jnp.float32)
    own_scale = lax.all_to_all(partial_scale, "dp", split_axis=0, concat_axis=1, tiled=True)
    scale_parts = [own_scale] + [shift(own_scale, offset) for offset in order]

    work = [(sample, local) for sample in range(samples) for local in range(heads_here)]
    arrived = []
    for sample, local in work:
        arrays = [array[sample] for array in (queries, keys, values, out_grad)]
        packed = pack(place_array, arrays, parts, heads_here, local)
        pieces = {offset: shift(packed[offset], offset) for offset in order}
        arrived.append([packed[0]] + [pieces[offset] for offset in range(1, parts)])
    back = []
    for index in range(len(work)):
        grads = attend(arrived[index])
        pieces = {offset: shift(grads[offset], parts - offset) for offset in order}
        back.append([grads[0]] + [pieces[offset] for offset in range(1, parts)])

    def after(arrays, index):
        if index >= len(back):
            return arrays
        arrays, back[index][0] = lax.optimization_barrier((arrays, back[index][0]))
        return arrays

    grad_parts = after(grad_parts, 0)
    scale_parts = after(scale_parts, len(back) - 1)
    summed_grad = sum(grad_parts)
    shares = lax.axis_size("dp")
    split_grad = summed_grad.reshape(samples * 2, shares, -1).transpose(1, 0, 2)
    owner_grad = lax.all_to_all(split_grad, "dp", split_axis=0, concat_axis=0, tiled=True)
    owner_grad = owner_grad.reshape(shares * samples, 2, -1)
    mod_scale = sum(scale_parts)
    text_hidden, text_grad = after((text_hidden, text_grad), len(back) - 1)
    hidden = text_hidden.astype(jnp.float32)
    incoming = text_grad.astype(jnp.float32)
    centred = hidden - jnp.mean(hidden, axis=-1, keepdims=True)
    inv_std = lax.rsqrt(jnp.mean(centred * centred, axis=-1, keepdims=True) + norm_eps)
    normed = centred * inv_std
    upstream = incoming * (1.0 + mod_scale[:, None, :])
    text_hidden_grad = inv_std * (
        upstream
        - jnp.mean(upstream, axis=-1, keepdims=True)
        - normed * jnp.mean(upstream * normed, axis=-1, keepdims=True)
    )
    text_hidden_grad = text_hidden_grad.astype(jnp.bfloat16)
    mod_weight_grad = jnp.einsum(
        "br,bkc->krc", act.astype(jnp.float32), owner_grad, precision=lax.Precision.HIGHEST
    )
    backward = jnp.einsum(
        "bkc,krc->br", owner_grad, mod_weight.astype(jnp.float32), precision=lax.Precision.HIGHEST
    )
    split_back = backward.reshape(shares, samples, -1)
    split_back = lax.all_to_all(split_back, "dp", split_axis=0, concat_axis=0, tiled=True)
    summed_back = jnp.sum(split_back, axis=0)
    sigma = jax.nn.sigmoid(cond_vec)
    cond_vec_grad = summed_back * sigma * (1.0 + cond_vec * (1.0 - sigma))

    joined = [None] * samples
    for index, (sample, local) in enumerate(work):
        joined[sample] = unpack(place_array, back[index], joined[sample], heads_here, local)
    query_grad, key_grad, value_grad = (
        jnp.stack([joined[sample][which] for sample in range(samples)]) for which in range(3)
    )
    return (text_hidden_grad, mod_weight_grad, cond_vec_grad, query_grad, key_grad, value_grad)


def solution(mesh):
    return jax.shard_map(
        per_device,
        mesh=mesh,
        in_specs=(
            P("dp", "seq"),
            P(None, "seq", "dp"),
            P("dp", "seq", None),
            P("dp", "seq", None),
            P("dp", "seq", None),
            P("dp", "seq", None),
            P("dp", "seq", None),
            P("dp", "seq", None),
        ),
        out_specs=(
            P("dp", "seq", None),
            P(None, "seq", "dp"),
            P("dp", "seq"),
            P("dp", "seq", None),
            P("dp", "seq", None),
            P("dp", "seq", None),
        ),
        check_vma=False,
    )
```
